32 devices in a mesh: dev: 32 (over z, y, x, core).
Axes of the slice: x: 2, y: 2, z: 4, core: 2. Of those that a mesh axis runs over, the one named last changes fastest.
Arguments:
- features: bfloat16 [16384, 1024], P('dev'), may hold values from -6 to 6
- w_hidden: bfloat16 [1024, 512], replicated, may hold values from -0.1875 to 0.1875
- w_out: bfloat16 [512, 128], replicated, may hold values from -0.25 to 0.25
- items: bfloat16 [65536, 128], P('dev'), may hold values from -200 to 200
- routes: int32 [16384, 4], P('dev'), may hold values from 0 to 511, all different within a row; in each aligned block of 512 rows (0 to 511, 512 to 1023, ...) at most 8 rows name the same one
- cluster_slot: int32 [512], replicated, may hold values from 0 to 511, each once
- sample_ids: int32 [512, 4096], P('dev'), may hold values from 0 to 127
- sample_counts: int32 [512, 4096], P('dev'), may hold values from 1 to 4095
- positives: int32 [16384, 4], P('dev'), may hold values from 0 to 4095
Outputs:
- slot_loss: float32 [512], P('dev')
- grad_hidden: float32 [1024, 512], replicated
- grad_out: float32 [512, 128], replicated
- item_grad: float32 [65536, 128], P('dev')
The draws below stay inside these ranges and needn't reach their ends.
Inputs may be any that keep to these rules, and one draw needn't show every extreme that they name: `routes`: each row names 4 different clusters; within the rows of one device no cluster is named more than 8 times; every cluster is named by some row. `cluster_slot`: each cluster has one slot.
All inputs are finite; a program needn't handle non-finite values.
Results may differ from the reference program's by a relative error of at most 0.012.
The reference program's roundings to bfloat16 on the way (of `hidden`, `query`, `weight`, `dquery`, `dq_total` and `dpre`) count: a program that leaves them out, or rounds other values in their place, can miss the bound.
Values may be sent and summed in bfloat16 or wider, within the bound.
A program may use at most 128 MiB of HBM per device.

```python
import math
import jax
import jax.numpy as jnp
import numpy as np
from jax import lax

FEAT = 1024
HID = 512
EMB = 128
ROUTES = 4
U_DEV = 512
CL_DEV = 16
SAMPLES = 4096
ITEM_CL = 128
ITEM_DEV = 2048
USERS = 16384
CLUSTERS = 512
CAP = 8
ITEMS = 65536
N_DEV = 32


def draw_items(key, part):
    keys = jax.random.split(jax.random.fold_in(key, 17), 1)
    base = jax.random.normal(keys[0], (ITEMS, EMB), jnp.float32) * EMB ** (-0.5)
    return base.astype(jnp.bfloat16)


def place_ends(drawn, own_key, smallest, high):
    longest = drawn.shape.index(max(drawn.shape))
    spots = []
    for shift in (0, 1):
        where = [jax.random.randint(jax.random.fold_in(own_key, axis), (), 0, length) for axis, length in enumerate(drawn.shape)]
        where[longest] = (where[longest] + shift) % drawn.shape[longest]
        spots.append(tuple(where))
    return drawn.at[spots[0]].set(smallest).at[spots[1]].set(high)


def block_levels(own_key, shape, cuts, smallest, top_value):
    def one(axis_at, parts):
        heights = jax.random.uniform(jax.random.fold_in(jax.random.fold_in(own_key, 6), axis_at), (parts,), jnp.float32, smallest / len(cuts), top_value / len(cuts))
        return jnp.repeat(jnp.exp(heights), shape[axis_at] // parts).reshape((-1,) + (1,) * (len(shape) - axis_at - 1))

    gain = one(*cuts[0])
    for cut in cuts[1:]:
        gain = gain * one(*cut)
    return gain


def assign_block(key, own, number, rows, amount, top, bound, lean):
    order = jax.random.permutation(key, amount)
    packed, usual = portions_of(amount, rows * top, bound, lean, True), portions_of(amount, rows * top, bound, lean, False)
    places = jnp.arange(amount)

    def named(sizes, rotation):
        used = int((sizes > 0).sum())
        fixed = max(1, used // 4)
        shifted = fixed + (places - fixed + rotation * (used - fixed)) % max(1, amount - fixed)
        return jnp.zeros((amount,), jnp.int32).at[order[jnp.where(places < fixed, places, shifted)]].set(jnp.asarray(sizes, jnp.int32))

    sizes = jnp.where(number % 4 == 0, named(packed, number // 4), named(usual, number - number // 4 - 1))
    mixed = jax.random.permutation(jax.random.fold_in(own, 3), amount)
    giver, taker = mixed[0:amount // 2 * 2:2], mixed[1:amount // 2 * 2:2]
    slack = jnp.minimum(sizes[giver] - 1, bound - sizes[taker]) // 2
    slack = jnp.where((giver == order[0]) | (taker == order[0]) | (sizes[taker] == 0), 0, jnp.maximum(slack, 0))
    shifted = jax.random.randint(jax.random.fold_in(own, 4), (amount // 2,), 0, 1 << 20) % (slack + 1)
    sizes = sizes.at[giver].add(-shifted).at[taker].add(shifted)
    labels = jnp.searchsorted(jnp.cumsum(sizes), jnp.arange(rows * top), side="right").astype(jnp.int32)
    grid = labels.reshape(top, rows).T
    grid = grid[jax.random.permutation(jax.random.fold_in(own, 1), rows)]
    rotation = jax.random.randint(jax.random.fold_in(own, 2), (rows, 1), 0, top)
    return jnp.take_along_axis(grid, (jnp.arange(top)[None, :] + rotation) % top, axis=1)


def portions_of(amount, total, bound, slope, full):
    loads = [(1 << 20) // math.isqrt(standing ** slope) + 1 for standing in range(1, amount + 1)]
    largest = bound if full else min(bound, max(-(-total // amount), total * loads[0] // sum(loads)))
    least = 1 if total - largest >= amount - 1 else 0
    holding, spare = [largest] + [least] * (amount - 1), total - largest - least * (amount - 1)
    while spare > 0:
        free = [i for i in range(1, amount) if holding[i] < largest] or [i for i in range(1, amount) if holding[i] < bound]
        whole, left = sum([loads[i] for i in free]), spare
        for i in free:
            more = min(bound - holding[i], max(1, left * loads[i] // whole), spare)
            holding[i] = holding[i] + more
            spare = spare - more
    return np.array(holding)


def gaussian(stream_key, extent, spread, limit, shards=(), kind=jnp.bfloat16):
    array = jax.random.normal(stream_key, extent, jnp.float32) * spread
    if len(shards) > 0:
        array = block_levels(stream_key, extent, shards, -0.22, 0.18) * array
    return jnp.clip(array, min=-limit, max=limit).astype(kind)


def setup_inputs(seed: int = 0) -> dict:
    arg_keys = jax.random.split(jax.random.key(seed), 10)
    features = gaussian(arg_keys[0], (USERS, FEAT), 1.0, 6.0, ((0, 32),))
    w_hidden = gaussian(arg_keys[1], (FEAT, HID), FEAT ** -0.5, 0.1875)
    w_out = gaussian(arg_keys[2], (HID, EMB), HID ** -0.5, 0.25)
    items = draw_items(jax.random.fold_in(arg_keys[9], 71), 0)
    routes_keys = jax.random.split(jax.random.fold_in(arg_keys[4], 1), USERS // U_DEV)
    routes_turns = jax.random.permutation(jax.random.fold_in(arg_keys[4], 3), USERS // U_DEV)
    routes = jax.vmap(lambda own, number: assign_block(jax.random.fold_in(arg_keys[4], 2), own, number, U_DEV, CLUSTERS, ROUTES, CAP, 2))(routes_keys, routes_turns).reshape((USERS, ROUTES))
    cluster_slot = jax.random.permutation(arg_keys[5], CLUSTERS).astype(jnp.int32)
    sample_ids = place_ends(jax.random.randint(arg_keys[6], (CLUSTERS, SAMPLES), 0, ITEM_CL), jax.random.fold_in(arg_keys[6], 1), 0, ITEM_CL - 1).astype(jnp.int32)
    sample_counts = place_ends(jax.random.randint(arg_keys[7], (CLUSTERS, SAMPLES), 1, 4096), jax.random.fold_in(arg_keys[7], 1), 1, 4095).astype(jnp.int32)
    positives = place_ends(jax.random.randint(arg_keys[8], (USERS, ROUTES), 0, SAMPLES), jax.random.fold_in(arg_keys[8], 1), 0, SAMPLES - 1).astype(jnp.int32)
    return dict(features=features, w_hidden=w_hidden, w_out=w_out, items=items, routes=routes, cluster_slot=cluster_slot, sample_ids=sample_ids, sample_counts=sample_counts, positives=positives)


def silu_grad(value):
    sig = jax.nn.sigmoid(value)
    return sig * (1.0 + value * (1.0 - sig))

def slot_ranks(keys):
    order = jnp.argsort(keys, stable=True).astype(jnp.int32)
    sorted_keys = keys[order]
    first = jnp.searchsorted(sorted_keys, sorted_keys, side='left').astype(jnp.int32)
    ranked = jnp.arange(keys.shape[0], dtype=jnp.int32) - first
    return jnp.zeros_like(keys).at[order].set(ranked)

def score_block(queries, targets, table, counts):
    scores = jnp.einsum('cqe,cse->cqs', queries.astype(jnp.float32), table.astype(jnp.float32))
    scores = scores - jnp.log(counts.astype(jnp.float32))[:, None, :]
    top = lax.optimization_barrier(jnp.max(scores, axis=2, keepdims=True))
    expo = jnp.exp(scores - top)
    total = lax.optimization_barrier(jnp.sum(expo, axis=2, keepdims=True))
    hit = lax.broadcasted_iota(jnp.int32, scores.shape, 2) == targets[:, :, None]
    picked = lax.optimization_barrier(jnp.sum(jnp.where(hit, scores, 0.0), axis=2))
    losses = jnp.log(total[:, :, 0]) + top[:, :, 0] - picked
    live = targets >= 0
    cluster_loss = lax.optimization_barrier(jnp.sum(jnp.where(live, losses, 0.0), axis=1)) / lax.optimization_barrier(jnp.sum(live.astype(jnp.float32), axis=1))
    weight = (expo / total - hit.astype(jnp.float32)).astype(jnp.bfloat16)
    dquery = jnp.einsum('cqs,cse->cqe', weight.astype(jnp.float32), table.astype(jnp.float32)).astype(jnp.bfloat16)
    dtable = jnp.einsum('cqs,cqe->cse', weight.astype(jnp.float32), queries.astype(jnp.float32))
    return (cluster_loss, dquery, dtable)

def pick_rows(block, ids):
    return block[ids]

def sum_rows(values, ids):
    return jax.ops.segment_sum(values, ids, num_segments=ITEM_CL)

def reference(features, w_hidden, w_out, items, routes, cluster_slot, sample_ids, sample_counts, positives):
    pre = jnp.dot(features, w_hidden, preferred_element_type=jnp.float32)
    hidden = jax.nn.silu(pre).astype(jnp.bfloat16)
    query = jnp.dot(hidden, w_out, preferred_element_type=jnp.float32).astype(jnp.bfloat16)
    users = features.shape[0]
    slots = cluster_slot[routes]
    source = jnp.broadcast_to((jnp.arange(users, dtype=jnp.int32) // U_DEV)[:, None], slots.shape)
    keys = (source * CLUSTERS + slots).reshape(-1)
    ranks = slot_ranks(keys)
    column = source.reshape(-1) * CAP + ranks
    row = slots.reshape(-1)
    width = N_DEV * CAP
    qbuf = jnp.zeros((CLUSTERS, width, EMB), jnp.bfloat16).at[row, column].set(jnp.repeat(query, ROUTES, axis=0))
    tbuf = jnp.full((CLUSTERS, width), -1, jnp.int32).at[row, column].set(positives.reshape(-1))

    def owner(carry, index):
        start = (index * CL_DEV).astype(jnp.int32)
        queries = lax.dynamic_slice_in_dim(qbuf, start, CL_DEV, 0)
        targets = lax.dynamic_slice_in_dim(tbuf, start, CL_DEV, 0)
        table_ids = lax.dynamic_slice_in_dim(sample_ids, start, CL_DEV, 0)
        counts = lax.dynamic_slice_in_dim(sample_counts, start, CL_DEV, 0)
        block_rows = lax.dynamic_slice_in_dim(items, (index * ITEM_DEV).astype(jnp.int32), ITEM_DEV, 0)
        block_rows = block_rows.reshape(CL_DEV, ITEM_CL, EMB)
        table = jax.vmap(pick_rows)(block_rows, table_ids)
        cluster_loss, dquery, dtable = score_block(queries, targets, table, counts)
        grads = jax.vmap(sum_rows)(dtable, table_ids)
        return (carry, (cluster_loss, dquery, grads))
    _, (losses, dqbuf, igrad) = lax.scan(owner, jnp.zeros((), jnp.float32), jnp.arange(N_DEV, dtype=jnp.int32))
    slot_loss = losses.reshape(-1)
    item_grad = igrad.reshape(ITEMS, EMB)
    dq_pairs = dqbuf.reshape(CLUSTERS, width, EMB)[row, column].astype(jnp.float32).reshape(users, ROUTES, EMB)
    dq_total = lax.optimization_barrier(jnp.sum(dq_pairs, axis=1)).astype(jnp.bfloat16)
    grad_out = jnp.dot(hidden.T, dq_total, preferred_element_type=jnp.float32)
    dhidden = jnp.dot(dq_total, w_out.T, preferred_element_type=jnp.float32)
    dpre = (dhidden * silu_grad(pre)).astype(jnp.bfloat16)
    grad_hidden = jnp.dot(features.T, dpre, preferred_element_type=jnp.float32)
    return (slot_loss, grad_hidden, grad_out, item_grad)
```

```python
import jax
import jax.numpy as jnp
from jax import lax
from jax.sharding import PartitionSpec as P


def silu_grad(value):
    sig = jax.nn.sigmoid(value)
    return sig * (1.0 + value * (1.0 - sig))


def slot_codes(routes_t, positives_t, cluster_slot, capacity):
    visits, users = routes_t.shape
    clusters = cluster_slot.shape[0]
    ids = lax.broadcasted_iota(jnp.int32, (visits, clusters, users), 1)
    slots = jnp.sum(
        jnp.where(routes_t[:, None, :] == ids, cluster_slot[None, :, None], 0), axis=1
    )
    rows = lax.broadcasted_iota(jnp.int32, (clusters, users), 0)
    member = jnp.zeros((clusters, users), jnp.bool_)
    target = jnp.zeros((clusters, users), jnp.int32)
    for r in range(visits):
        same = slots[r][None, :] == rows
        member = member | same
        target = jnp.where(same, positives_t[r][None, :] + 1, target)
    earlier = lax.broadcasted_iota(jnp.int32, (users, users), 0) < lax.broadcasted_iota(
        jnp.int32, (users, users), 1
    )
    rank = jnp.dot(
        member.astype(jnp.bfloat16),
        earlier.astype(jnp.bfloat16),
        preferred_element_type=jnp.float32,
    )
    code = jnp.where(member, rank, -1.0).astype(jnp.bfloat16)
    return code, target


def owner(queries, targets, block_items, table_ids, counts):
    clusters, samples = table_ids.shape
    item_rows = block_items.shape[1]
    recip = 1.0 / counts.astype(jnp.float32)
    which = lax.broadcasted_iota(jnp.int32, (clusters, item_rows, samples), 1)
    mass = jnp.sum(jnp.where(table_ids[:, None, :] == which, recip[:, None, :], 0.0), axis=2)
    log_mass = jnp.log(mass)
    lanes = 128
    groups = samples // lanes
    low = targets % lanes
    high = targets // lanes
    pick_low = (
        low[:, :, None] == lax.broadcasted_iota(jnp.int32, low.shape + (lanes,), 2)
    ).astype(jnp.bfloat16)
    table = jnp.concatenate([table_ids, counts // 64, counts % 64], axis=1)
    table = table.reshape(clusters, 3 * groups, lanes).astype(jnp.bfloat16)
    near = jnp.einsum("cql,chl->cqh", pick_low, table, preferred_element_type=jnp.float32)
    column = lax.broadcasted_iota(jnp.int32, near.shape, 2)
    parts = [
        jnp.sum(jnp.where(column == high[:, :, None] + groups * t, near, 0.0), axis=2)
        for t in range(3)
    ]
    live = targets >= 0
    own_id = parts[0].astype(jnp.int32)
    own_count = jnp.where(live, parts[1] * 64.0 + parts[2], 1.0)
    scores = jnp.einsum("cqe,cie->cqi", queries, block_items, preferred_element_type=jnp.float32)
    shifted = scores + log_mass[:, None, :]
    top = jnp.max(shifted, axis=2, keepdims=True)
    expo = jnp.exp(shifted - top)
    total = jnp.sum(expo, axis=2, keepdims=True)
    hit = (
        lax.broadcasted_iota(jnp.int32, scores.shape, 2)
        == jnp.where(live, own_id, -1)[:, :, None]
    )
    picked = jnp.sum(jnp.where(hit, scores, 0.0), axis=2) - jnp.log(own_count)
    losses = jnp.log(total[:, :, 0]) + top[:, :, 0] - picked
    cluster_loss = jnp.sum(jnp.where(live, losses, 0.0), axis=1) / jnp.sum(
        live.astype(jnp.float32), axis=1
    )
    wsum = expo / total - hit.astype(jnp.float32)
    coarse = lax.reduce_precision(wsum, 8, 7)
    fine = (wsum - coarse).astype(jnp.bfloat16)
    coarse = coarse.astype(jnp.bfloat16)

    def both(equation, other):
        return jnp.einsum(
            equation, coarse, other, preferred_element_type=jnp.float32
        ) + jnp.einsum(equation, fine, other, preferred_element_type=jnp.float32)

    dquery = both("cqi,cie->cqe", block_items).astype(jnp.bfloat16)
    dtable = both("cqi,cqe->cie", queries)
    return cluster_loss, dquery, dtable


def local(
    features, w_hidden, w_out, items, routes, cluster_slot, sample_ids, sample_counts, positives
):
    devices = lax.axis_size("dev")
    users, visits = routes.shape
    clusters = cluster_slot.shape[0]
    local_clusters = sample_ids.shape[0]
    width = w_out.shape[1]
    item_rows = items.shape[0] // local_clusters
    capacity = max(2, 2 * users * visits // (local_clusters * devices))
    rows = local_clusters * capacity
    code, target = slot_codes(routes.T, positives.T, cluster_slot, capacity)
    seats = lax.broadcasted_iota(jnp.int32, (1, capacity, 1), 1).astype(jnp.bfloat16)
    seated = code[:, None, :] == seats
    select = seated.astype(jnp.bfloat16).reshape(clusters * capacity, users)
    send_target = jnp.sum(jnp.where(seated, target[:, None, :], 0), axis=2)
    send_target = send_target.reshape(devices, rows)
    coded = jnp.concatenate([send_target // 64, send_target % 64], axis=1)
    extra = -(-coded.shape[1] // (16 * width)) * 16
    coded = jnp.pad(coded, ((0, 0), (0, extra * width - coded.shape[1])))
    coded = coded.astype(jnp.bfloat16).reshape(devices, extra, width)
    pre = jnp.dot(features, w_hidden, preferred_element_type=jnp.float32)
    hidden = jax.nn.silu(pre).astype(jnp.bfloat16)
    query = jnp.dot(hidden, w_out, preferred_element_type=jnp.float32).astype(jnp.bfloat16)
    send_query = jnp.dot(select, query, preferred_element_type=jnp.float32).astype(jnp.bfloat16)
    payload = jnp.concatenate([send_query.reshape(devices, rows, width), coded], axis=1)
    got = lax.all_to_all(payload, "dev", split_axis=0, concat_axis=0, tiled=True)
    got_query = got[:, :rows].reshape(devices, local_clusters, capacity, width)
    got_query = got_query.transpose(1, 0, 2, 3).reshape(local_clusters, devices * capacity, width)
    got_coded = got[:, rows:].reshape(devices, extra * width).astype(jnp.int32)
    got_target = got_coded[:, :rows] * 64 + got_coded[:, rows : 2 * rows] - 1
    got_target = got_target.reshape(devices, local_clusters, capacity)
    got_target = got_target.transpose(1, 0, 2).reshape(local_clusters, devices * capacity)
    slot_loss, dquery, dtable = owner(
        got_query,
        got_target,
        items.reshape(local_clusters, item_rows, width),
        sample_ids,
        sample_counts,
    )
    back = dquery.reshape(local_clusters, devices, capacity, width).transpose(1, 0, 2, 3)
    returned = lax.all_to_all(
        back.reshape(devices, rows, width), "dev", split_axis=0, concat_axis=0, tiled=True
    ).reshape(clusters * capacity, width)
    dq_total = lax.dot_general(
        select, returned, (((0,), (0,)), ((), ())), preferred_element_type=jnp.float32
    ).astype(jnp.bfloat16)
    local_out = jnp.dot(hidden.T, dq_total, preferred_element_type=jnp.float32)
    dhidden = jnp.dot(dq_total, w_out.T, preferred_element_type=jnp.float32)
    dpre = (dhidden * silu_grad(pre)).astype(jnp.bfloat16)
    local_hidden = jnp.dot(features.T, dpre, preferred_element_type=jnp.float32)
    grad_hidden, grad_out = lax.psum((local_hidden, local_out), "dev")
    return (slot_loss, grad_hidden, grad_out, dtable.reshape(items.shape[0], width))


def solution(mesh):
    in_specs = (
        P("dev", None),
        P(),
        P(),
        P("dev", None),
        P("dev", None),
        P(),
        P("dev", None),
        P("dev", None),
        P("dev", None),
    )
    out_specs = (P("dev"), P(), P(), P("dev", None))
    return jax.shard_map(local, mesh=mesh, in_specs=in_specs, out_specs=out_specs, check_vma=False)
```

```python
import functools

import jax
import jax.numpy as jnp
from jax import lax
from jax.experimental import pallas as pl
from jax.experimental.pallas import tpu as pltpu
from jax.sharding import PartitionSpec as P


def silu_grad(value):
    sig = jax.nn.sigmoid(value)
    return sig * (1.0 + value * (1.0 - sig))


def slot_codes(routes_t, positives_t, cluster_slot, capacity):
    visits, users = routes_t.shape
    clusters = cluster_slot.shape[0]
    ids = lax.broadcasted_iota(jnp.int32, (visits, clusters, users), 1)
    slots = jnp.sum(
        jnp.where(routes_t[:, None, :] == ids, cluster_slot[None, :, None], 0), axis=1
    )
    rows = lax.broadcasted_iota(jnp.int32, (clusters, users), 0)
    member = jnp.zeros((clusters, users), jnp.bool_)
    target = jnp.zeros((clusters, users), jnp.int32)
    for r in range(visits):
        same = slots[r][None, :] == rows
        member = member | same
        target = jnp.where(same, positives_t[r][None, :] + 1, target)
    earlier = lax.broadcasted_iota(jnp.int32, (users, users), 0) < lax.broadcasted_iota(
        jnp.int32, (users, users), 1
    )
    rank = jnp.dot(
        member.astype(jnp.bfloat16),
        earlier.astype(jnp.bfloat16),
        preferred_element_type=jnp.float32,
    )
    code = jnp.where(member, rank, -1.0).astype(jnp.bfloat16)
    return code, target


def owner(queries, targets, block_items, table_ids, counts):
    clusters, samples = table_ids.shape
    item_rows = block_items.shape[1]
    recip = 1.0 / counts.astype(jnp.float32)
    which = lax.broadcasted_iota(jnp.int32, (clusters, item_rows, samples), 1)
    mass = jnp.sum(jnp.where(table_ids[:, None, :] == which, recip[:, None, :], 0.0), axis=2)
    log_mass = jnp.log(mass)
    lanes = 128
    groups = samples // lanes
    low = targets % lanes
    high = targets // lanes
    pick_low = (
        low[:, :, None] == lax.broadcasted_iota(jnp.int32, low.shape + (lanes,), 2)
    ).astype(jnp.bfloat16)
    table = jnp.concatenate([table_ids, counts // 64, counts % 64], axis=1)
    table = table.reshape(clusters, 3 * groups, lanes).astype(jnp.bfloat16)
    near = jnp.einsum("cql,chl->cqh", pick_low, table, preferred_element_type=jnp.float32)
    column = lax.broadcasted_iota(jnp.int32, near.shape, 2)
    parts = [
        jnp.sum(jnp.where(column == high[:, :, None] + groups * t, near, 0.0), axis=2)
        for t in range(3)
    ]
    live = targets >= 0
    own_id = parts[0].astype(jnp.int32)
    own_count = jnp.where(live, parts[1] * 64.0 + parts[2], 1.0)
    scores = jnp.einsum("cqe,cie->cqi", queries, block_items, preferred_element_type=jnp.float32)
    shifted = scores + log_mass[:, None, :]
    top = jnp.max(shifted, axis=2, keepdims=True)
    expo = jnp.exp(shifted - top)
    total = jnp.sum(expo, axis=2, keepdims=True)
    hit = (
        lax.broadcasted_iota(jnp.int32, scores.shape, 2)
        == jnp.where(live, own_id, -1)[:, :, None]
    )
    picked = jnp.sum(jnp.where(hit, scores, 0.0), axis=2) - jnp.log(own_count)
    losses = jnp.log(total[:, :, 0]) + top[:, :, 0] - picked
    cluster_loss = jnp.sum(jnp.where(live, losses, 0.0), axis=1) / jnp.sum(
        live.astype(jnp.float32), axis=1
    )
    wsum = expo / total - hit.astype(jnp.float32)
    coarse = lax.reduce_precision(wsum, 8, 7)
    fine = (wsum - coarse).astype(jnp.bfloat16)
    coarse = coarse.astype(jnp.bfloat16)

    def both(equation, other):
        return jnp.einsum(
            equation, coarse, other, preferred_element_type=jnp.float32
        ) + jnp.einsum(equation, fine, other, preferred_element_type=jnp.float32)

    dquery = both("cqi,cie->cqe", block_items).astype(jnp.bfloat16)
    dtable = both("cqi,cqe->cie", queries)
    return cluster_loss, dquery, dtable


LANES = 3


def bit_orders(bits):
    turn = [b for b in (1, 2, 3) if b < bits]
    rest = [b for b in range(bits) if b > 3]
    orders = []
    for lane in range(LANES):
        k = lane % max(1, len(turn))
        orders.append([0] + turn[k:] + turn[:k] + rest)
    return orders


def blocks_of(ref):
    rows, columns = ref.shape
    return [(c, rows) for c in range(columns // 128)]


def reduce_kernel(bits, unit, big_ref, small_ref, big_out, small_out, acc, out, inbox, full, send, recv):
    me = lax.axis_index("dev")
    mesh = pl.DeviceIdType.MESH
    orders = bit_orders(bits)
    per_lane = unit << bits
    partners = [me + (1 << b) * (1 - 2 * ((me // (1 << b)) % 2)) for b in range(bits)]
    bit = [(me // (1 << b)) % 2 for b in range(bits)]

    barrier = pltpu.get_barrier_semaphore()
    for b in range(bits):
        pl.semaphore_signal(barrier, inc=1, device_id=(partners[b],), device_id_type=mesh)
    row = 0
    for ref in (big_ref, small_ref):
        for c, rows in blocks_of(ref):
            acc[row : row + rows, :] = ref[:, c * 128 : (c + 1) * 128]
            row += rows
    if row < LANES * per_lane:
        acc[row:, :] = jnp.zeros((LANES * per_lane - row, 128), jnp.float32)

    off = [lane * per_lane for lane in range(LANES)]
    length = per_lane
    gap = []
    at = 0
    for s in range(bits):
        gap.append(at)
        at += per_lane >> (s + 1)
    started = []

    def rows_at(first, count):
        return pl.ds(pl.multiple_of(first, 16), count)

    for s in range(bits):
        half = length // 2
        copies = []
        for lane in range(LANES):
            b = orders[lane][s]
            give = off[lane] + (1 - bit[b]) * half
            off[lane] = off[lane] + bit[b] * half
            out[rows_at(give, half), :] = acc[rows_at(give, half), :].astype(jnp.bfloat16)
            if s == 0 and lane == 0:
                pl.semaphore_wait(barrier, bits)
            copy = pltpu.make_async_remote_copy(
                src_ref=out.at[rows_at(give, half), :],
                dst_ref=inbox.at[pl.ds(lane * per_lane + gap[s], half), :],
                send_sem=send.at[lane, s],
                recv_sem=recv.at[lane, s],
                device_id=(partners[b],),
                device_id_type=mesh,
            )
            copy.start()
            copies.append(copy)
            started.append(copy)
        for lane in range(LANES):
            copies[lane].wait_recv()
            kept = rows_at(off[lane], half)
            got = inbox[pl.ds(lane * per_lane + gap[s], half), :].astype(jnp.float32)
            acc[kept, :] = acc[kept, :] + got
        length = half
    for lane in range(LANES):
        kept = rows_at(off[lane], length)
        full[kept, :] = acc[kept, :].astype(jnp.bfloat16)
    for s in range(bits - 1, -1, -1):
        copies = []
        for lane in range(LANES):
            b = orders[lane][s]
            held = rows_at(off[lane], length)
            copy = pltpu.make_async_remote_copy(
                src_ref=full.at[held, :],
                dst_ref=full.at[held, :],
                send_sem=send.at[lane, bits + s],
                recv_sem=recv.at[lane, bits + s],
                device_id=(partners[b],),
                device_id_type=mesh,
            )
            copy.start()
            copies.append(copy)
            started.append(copy)
            off[lane] = off[lane] - bit[b] * length
        for lane in range(LANES):
            copies[lane].wait_recv()
        length = length * 2
    for copy in started:
        copy.wait_send()
    row = 0
    for ref in (big_out, small_out):
        for c, rows in blocks_of(ref):
            ref[:, c * 128 : (c + 1) * 128] = full[row : row + rows, :]
            row += rows


def sum_over_devices(big, small):
    devices = lax.axis_size("dev")
    bits = devices.bit_length() - 1
    total = (big.size + small.size) // 128
    unit = -(-total // (LANES * devices * 16)) * 16
    rows = LANES * devices * unit
    summed = pl.pallas_call(
        functools.partial(reduce_kernel, bits, unit),
        out_shape=(
            jax.ShapeDtypeStruct(big.shape, jnp.bfloat16),
            jax.ShapeDtypeStruct(small.shape, jnp.bfloat16),
        ),
        in_specs=[pl.BlockSpec(memory_space=pltpu.VMEM)] * 2,
        out_specs=[pl.BlockSpec(memory_space=pltpu.VMEM)] * 2,
        scratch_shapes=[
            pltpu.VMEM((rows, 128), jnp.float32),
            pltpu.VMEM((rows, 128), jnp.bfloat16),
            pltpu.VMEM((rows, 128), jnp.bfloat16),
            pltpu.VMEM((rows, 128), jnp.bfloat16),
            pltpu.SemaphoreType.DMA((LANES, 2 * bits)),
            pltpu.SemaphoreType.DMA((LANES, 2 * bits)),
        ],
        compiler_params=pltpu.CompilerParams(collective_id=0, has_side_effects=True),
        name="sum_over_devices",
    )(big, small)
    return tuple(part.astype(jnp.float32) for part in summed)


def local(
    features, w_hidden, w_out, items, routes, cluster_slot, sample_ids, sample_counts, positives
):
    devices = lax.axis_size("dev")
    users, visits = routes.shape
    clusters = cluster_slot.shape[0]
    local_clusters = sample_ids.shape[0]
    width = w_out.shape[1]
    item_rows = items.shape[0] // local_clusters
    capacity = max(2, 2 * users * visits // (local_clusters * devices))
    rows = local_clusters * capacity
    code, target = slot_codes(routes.T, positives.T, cluster_slot, capacity)
    seats = lax.broadcasted_iota(jnp.int32, (1, capacity, 1), 1).astype(jnp.bfloat16)
    seated = code[:, None, :] == seats
    select = seated.astype(jnp.bfloat16).reshape(clusters * capacity, users)
    send_target = jnp.sum(jnp.where(seated, target[:, None, :], 0), axis=2)
    send_target = send_target.reshape(devices, rows)
    coded = jnp.concatenate([send_target // 64, send_target % 64], axis=1)
    extra = -(-coded.shape[1] // (16 * width)) * 16
    coded = jnp.pad(coded, ((0, 0), (0, extra * width - coded.shape[1])))
    coded = coded.astype(jnp.bfloat16).reshape(devices, extra, width)
    pre = jnp.dot(features, w_hidden, preferred_element_type=jnp.float32)
    hidden = jax.nn.silu(pre).astype(jnp.bfloat16)
    query = jnp.dot(hidden, w_out, preferred_element_type=jnp.float32).astype(jnp.bfloat16)
    send_query = jnp.dot(select, query, preferred_element_type=jnp.float32).astype(jnp.bfloat16)
    payload = jnp.concatenate([send_query.reshape(devices, rows, width), coded], axis=1)
    got = lax.all_to_all(payload, "dev", split_axis=0, concat_axis=0, tiled=True)
    got_query = got[:, :rows].reshape(devices, local_clusters, capacity, width)
    got_query = got_query.transpose(1, 0, 2, 3).reshape(local_clusters, devices * capacity, width)
    got_coded = got[:, rows:].reshape(devices, extra * width).astype(jnp.int32)
    got_target = got_coded[:, :rows] * 64 + got_coded[:, rows : 2 * rows] - 1
    got_target = got_target.reshape(devices, local_clusters, capacity)
    got_target = got_target.transpose(1, 0, 2).reshape(local_clusters, devices * capacity)
    slot_loss, dquery, dtable = owner(
        got_query,
        got_target,
        items.reshape(local_clusters, item_rows, width),
        sample_ids,
        sample_counts,
    )
    back = dquery.reshape(local_clusters, devices, capacity, width).transpose(1, 0, 2, 3)
    returned = lax.all_to_all(
        back.reshape(devices, rows, width), "dev", split_axis=0, concat_axis=0, tiled=True
    ).reshape(clusters * capacity, width)
    dq_total = lax.dot_general(
        select, returned, (((0,), (0,)), ((), ())), preferred_element_type=jnp.float32
    ).astype(jnp.bfloat16)
    local_out = jnp.dot(hidden.T, dq_total, preferred_element_type=jnp.float32)
    dhidden = jnp.dot(dq_total, w_out.T, preferred_element_type=jnp.float32)
    dpre = (dhidden * silu_grad(pre)).astype(jnp.bfloat16)
    local_hidden = jnp.dot(features.T, dpre, preferred_element_type=jnp.float32)
    grad_hidden, grad_out = sum_over_devices(local_hidden, local_out)
    return (slot_loss, grad_hidden, grad_out, dtable.reshape(items.shape[0], width))


def solution(mesh):
    in_specs = (
        P("dev", None),
        P(),
        P(),
        P("dev", None),
        P("dev", None),
        P(),
        P("dev", None),
        P("dev", None),
        P("dev", None),
    )
    out_specs = (P("dev"), P(), P(), P("dev", None))
    return jax.shard_map(local, mesh=mesh, in_specs=in_specs, out_specs=out_specs, check_vma=False)
```

```python
import functools

import jax
import jax.numpy as jnp
from jax import lax
from jax.experimental import pallas as pl
from jax.experimental.pallas import tpu as pltpu
from jax.sharding import PartitionSpec as P


def silu_grad(value):
    sig = jax.nn.sigmoid(value)
    return sig * (1.0 + value * (1.0 - sig))


def slot_codes(routes_t, positives, cluster_slot, capacity):
    visits, users = routes_t.shape
    clusters = cluster_slot.shape[0]
    ids = lax.broadcasted_iota(jnp.int32, (visits, clusters, users), 1)
    slots = jnp.sum(
        jnp.where(routes_t[:, None, :] == ids, cluster_slot[None, :, None], 0), axis=1
    )
    rows = lax.broadcasted_iota(jnp.int32, (clusters, users), 0)
    columns = lax.broadcasted_iota(jnp.int32, (users, clusters), 1)
    slots_u = slots.T
    member = jnp.zeros((clusters, users), jnp.bool_)
    member_u = jnp.zeros((users, clusters), jnp.bool_)
    target_u = jnp.zeros((users, clusters), jnp.int32)
    for r in range(visits):
        member = member | (slots[r][None, :] == rows)
        same = slots_u[:, r][:, None] == columns
        member_u = member_u | same
        target_u = jnp.where(same, positives[:, r][:, None] + 1, target_u)
    first = lax.broadcasted_iota(jnp.int32, (users, users), 0)
    second = lax.broadcasted_iota(jnp.int32, (users, users), 1)
    rank = jnp.dot(
        member.astype(jnp.bfloat16),
        (first < second).astype(jnp.bfloat16),
        preferred_element_type=jnp.float32,
    )
    rank_u = jnp.dot(
        (second < first).astype(jnp.bfloat16),
        member_u.astype(jnp.bfloat16),
        preferred_element_type=jnp.float32,
    )
    code = jnp.where(member, rank, -1.0).astype(jnp.bfloat16)
    code_u = jnp.where(member_u, rank_u, -1.0)
    seats = [
        jnp.sum(jnp.where(code_u == k, target_u, 0), axis=0) for k in range(capacity)
    ]
    return code, jnp.stack(seats)


def owner(queries, targets, block_items, table_ids, counts):
    clusters, samples = table_ids.shape
    item_rows = block_items.shape[1]
    recip = 1.0 / counts.astype(jnp.float32)
    which = lax.broadcasted_iota(jnp.int32, (clusters, item_rows, samples), 1)
    mass = jnp.sum(jnp.where(table_ids[:, None, :] == which, recip[:, None, :], 0.0), axis=2)
    log_mass = jnp.log(mass)
    lanes = 128
    groups = samples // lanes
    low = targets % lanes
    high = targets // lanes
    pick_low = (
        low[:, :, None] == lax.broadcasted_iota(jnp.int32, low.shape + (lanes,), 2)
    ).astype(jnp.bfloat16)
    table = jnp.concatenate([table_ids, counts // 64, counts % 64], axis=1)
    table = table.reshape(clusters, 3 * groups, lanes).astype(jnp.bfloat16)
    near = jnp.einsum("cql,chl->cqh", pick_low, table, preferred_element_type=jnp.float32)
    column = lax.broadcasted_iota(jnp.int32, near.shape, 2)
    parts = [
        jnp.sum(jnp.where(column == high[:, :, None] + groups * t, near, 0.0), axis=2)
        for t in range(3)
    ]
    live = targets >= 0
    own_id = parts[0].astype(jnp.int32)
    own_count = jnp.where(live, parts[1] * 64.0 + parts[2], 1.0)
    scores = jnp.einsum("cqe,cie->cqi", queries, block_items, preferred_element_type=jnp.float32)
    shifted = scores + log_mass[:, None, :]
    top = jnp.max(shifted, axis=2, keepdims=True)
    expo = jnp.exp(shifted - top)
    total = jnp.sum(expo, axis=2, keepdims=True)
    hit = (
        lax.broadcasted_iota(jnp.int32, scores.shape, 2)
        == jnp.where(live, own_id, -1)[:, :, None]
    )
    picked = jnp.sum(jnp.where(hit, scores, 0.0), axis=2) - jnp.log(own_count)
    losses = jnp.log(total[:, :, 0]) + top[:, :, 0] - picked
    cluster_loss = jnp.sum(jnp.where(live, losses, 0.0), axis=1) / jnp.sum(
        live.astype(jnp.float32), axis=1
    )
    wsum = expo / total - hit.astype(jnp.float32)
    coarse = lax.reduce_precision(wsum, 8, 7)
    fine = (wsum - coarse).astype(jnp.bfloat16)
    coarse = coarse.astype(jnp.bfloat16)

    def both(equation, other):
        return jnp.einsum(
            equation, coarse, other, preferred_element_type=jnp.float32
        ) + jnp.einsum(equation, fine, other, preferred_element_type=jnp.float32)

    dquery = both("cqi,cie->cqe", block_items).astype(jnp.bfloat16)
    dtable = both("cqi,cqe->cie", queries)
    return cluster_loss, dquery, dtable


LANES = 3


def bit_orders(bits):
    turn = [b for b in (1, 2, 3) if b < bits]
    rest = [b for b in range(bits) if b > 3]
    orders = []
    for lane in range(LANES):
        k = lane % max(1, len(turn))
        orders.append([0] + turn[k:] + turn[:k] + rest)
    return orders


def blocks_of(ref):
    rows, columns = ref.shape
    return [(c, rows) for c in range(columns // 128)]


def reduce_kernel(bits, unit, big_ref, small_ref, big_out, small_out, acc, out, inbox, full, send, recv):
    me = lax.axis_index("dev")
    mesh = pl.DeviceIdType.MESH
    orders = bit_orders(bits)
    per_lane = unit << bits
    partners = [me + (1 << b) * (1 - 2 * ((me // (1 << b)) % 2)) for b in range(bits)]
    bit = [(me // (1 << b)) % 2 for b in range(bits)]

    barrier = pltpu.get_barrier_semaphore()
    for b in range(bits):
        pl.semaphore_signal(barrier, inc=1, device_id=(partners[b],), device_id_type=mesh)
    row = 0
    for ref in (big_ref, small_ref):
        for c, rows in blocks_of(ref):
            acc[row : row + rows, :] = ref[:, c * 128 : (c + 1) * 128]
            row += rows
    if row < LANES * per_lane:
        acc[row:, :] = jnp.zeros((LANES * per_lane - row, 128), jnp.float32)

    off = [lane * per_lane for lane in range(LANES)]
    length = per_lane
    gap = []
    at = 0
    for s in range(bits):
        gap.append(at)
        at += per_lane >> (s + 1)
    started = []

    def rows_at(first, count):
        return pl.ds(pl.multiple_of(first, 16), count)

    for s in range(bits):
        half = length // 2
        copies = []
        for lane in range(LANES):
            b = orders[lane][s]
            give = off[lane] + (1 - bit[b]) * half
            off[lane] = off[lane] + bit[b] * half
            out[rows_at(give, half), :] = acc[rows_at(give, half), :].astype(jnp.bfloat16)
            if s == 0 and lane == 0:
                pl.semaphore_wait(barrier, bits)
            copy = pltpu.make_async_remote_copy(
                src_ref=out.at[rows_at(give, half), :],
                dst_ref=inbox.at[pl.ds(lane * per_lane + gap[s], half), :],
                send_sem=send.at[lane, s],
                recv_sem=recv.at[lane, s],
                device_id=(partners[b],),
                device_id_type=mesh,
            )
            copy.start()
            copies.append(copy)
            started.append(copy)
        for lane in range(LANES):
            copies[lane].wait_recv()
            kept = rows_at(off[lane], half)
            got = inbox[pl.ds(lane * per_lane + gap[s], half), :].astype(jnp.float32)
            acc[kept, :] = acc[kept, :] + got
        length = half
    for lane in range(LANES):
        kept = rows_at(off[lane], length)
        full[kept, :] = acc[kept, :].astype(jnp.bfloat16)
    for s in range(bits - 1, -1, -1):
        copies = []
        for lane in range(LANES):
            b = orders[lane][s]
            held = rows_at(off[lane], length)
            copy = pltpu.make_async_remote_copy(
                src_ref=full.at[held, :],
                dst_ref=full.at[held, :],
                send_sem=send.at[lane, bits + s],
                recv_sem=recv.at[lane, bits + s],
                device_id=(partners[b],),
                device_id_type=mesh,
            )
            copy.start()
            copies.append(copy)
            started.append(copy)
            off[lane] = off[lane] - bit[b] * length
        for lane in range(LANES):
            copies[lane].wait_recv()
        length = length * 2
    for copy in started:
        copy.wait_send()
    row = 0
    for ref in (big_out, small_out):
        for c, rows in blocks_of(ref):
            ref[:, c * 128 : (c + 1) * 128] = full[row : row + rows, :]
            row += rows


def sum_over_devices(big, small):
    devices = lax.axis_size("dev")
    bits = devices.bit_length() - 1
    total = (big.size + small.size) // 128
    unit = -(-total // (LANES * devices * 16)) * 16
    rows = LANES * devices * unit
    summed = pl.pallas_call(
        functools.partial(reduce_kernel, bits, unit),
        out_shape=(
            jax.ShapeDtypeStruct(big.shape, jnp.bfloat16),
            jax.ShapeDtypeStruct(small.shape, jnp.bfloat16),
        ),
        in_specs=[pl.BlockSpec(memory_space=pltpu.VMEM)] * 2,
        out_specs=[pl.BlockSpec(memory_space=pltpu.VMEM)] * 2,
        scratch_shapes=[
            pltpu.VMEM((rows, 128), jnp.float32),
            pltpu.VMEM((rows, 128), jnp.bfloat16),
            pltpu.VMEM((rows, 128), jnp.bfloat16),
            pltpu.VMEM((rows, 128), jnp.bfloat16),
            pltpu.SemaphoreType.DMA((LANES, 2 * bits)),
            pltpu.SemaphoreType.DMA((LANES, 2 * bits)),
        ],
        compiler_params=pltpu.CompilerParams(collective_id=0, has_side_effects=True),
        name="sum_over_devices",
    )(big, small)
    return tuple(part.astype(jnp.float32) for part in summed)


def local(
    features, w_hidden, w_out, items, routes, cluster_slot, sample_ids, sample_counts, positives
):
    devices = lax.axis_size("dev")
    users, visits = routes.shape
    clusters = cluster_slot.shape[0]
    local_clusters = sample_ids.shape[0]
    width = w_out.shape[1]
    item_rows = items.shape[0] // local_clusters
    capacity = max(2, 2 * users * visits // (local_clusters * devices))
    rows = local_clusters * capacity
    code, send_target = slot_codes(routes.T, positives, cluster_slot, capacity)
    seats = lax.broadcasted_iota(jnp.int32, (1, capacity, 1), 1).astype(jnp.bfloat16)
    seated = code[:, None, :] == seats
    select = seated.astype(jnp.bfloat16).reshape(clusters * capacity, users)
    send_target = send_target.reshape(capacity, devices, local_clusters)
    send_target = send_target.transpose(1, 0, 2).reshape(devices, rows)
    coded = jnp.concatenate([send_target // 64, send_target % 64], axis=1)
    extra = -(-coded.shape[1] // (8 * width)) * 8
    coded = jnp.pad(coded, ((0, 0), (0, extra * width - coded.shape[1])))
    coded = coded.astype(jnp.bfloat16).reshape(devices, extra, width)
    pre = jnp.dot(features, w_hidden, preferred_element_type=jnp.float32)
    hidden = jax.nn.silu(pre).astype(jnp.bfloat16)
    query = jnp.dot(hidden, w_out, preferred_element_type=jnp.float32).astype(jnp.bfloat16)
    send_query = jnp.dot(select, query, preferred_element_type=jnp.float32).astype(jnp.bfloat16)
    payload = jnp.concatenate([send_query.reshape(devices, rows, width), coded], axis=1)
    got = lax.all_to_all(payload, "dev", split_axis=0, concat_axis=0, tiled=True)
    got_query = got[:, :rows].reshape(devices, local_clusters, capacity, width)
    got_query = got_query.transpose(1, 0, 2, 3).reshape(local_clusters, devices * capacity, width)
    got_coded = got[:, rows:].reshape(devices, extra * width).astype(jnp.int32)
    got_target = got_coded[:, :rows] * 64 + got_coded[:, rows : 2 * rows] - 1
    got_target = got_target.reshape(devices, capacity, local_clusters)
    got_target = got_target.transpose(2, 0, 1).reshape(local_clusters, devices * capacity)
    slot_loss, dquery, dtable = owner(
        got_query,
        got_target,
        items.reshape(local_clusters, item_rows, width),
        sample_ids,
        sample_counts,
    )
    back = dquery.reshape(local_clusters, devices, capacity, width).transpose(1, 0, 2, 3)
    returned = lax.all_to_all(
        back.reshape(devices, rows, width), "dev", split_axis=0, concat_axis=0, tiled=True
    ).reshape(clusters * capacity, width)
    dq_total = lax.dot_general(
        select, returned, (((0,), (0,)), ((), ())), preferred_element_type=jnp.float32
    ).astype(jnp.bfloat16)
    local_out = jnp.dot(hidden.T, dq_total, preferred_element_type=jnp.float32)
    dhidden = jnp.dot(dq_total, w_out.T, preferred_element_type=jnp.float32)
    dpre = (dhidden * silu_grad(pre)).astype(jnp.bfloat16)
    local_hidden = jnp.dot(features.T, dpre, preferred_element_type=jnp.float32)
    grad_hidden, grad_out = sum_over_devices(local_hidden, local_out)
    return (slot_loss, grad_hidden, grad_out, dtable.reshape(items.shape[0], width))


def solution(mesh):
    in_specs = (
        P("dev", None),
        P(),
        P(),
        P("dev", None),
        P("dev", None),
        P(),
        P("dev", None),
        P("dev", None),
        P("dev", None),
    )
    out_specs = (P("dev"), P(), P(), P("dev", None))
    return jax.shard_map(local, mesh=mesh, in_specs=in_specs, out_specs=out_specs, check_vma=False)
```

```python
import functools

import jax
import jax.numpy as jnp
from jax import lax
from jax.experimental import pallas as pl
from jax.experimental.pallas import tpu as pltpu
from jax.sharding import PartitionSpec as P


def silu_grad(value):
    sig = jax.nn.sigmoid(value)
    return sig * (1.0 + value * (1.0 - sig))


def slot_codes(routes_t, positives, cluster_slot, capacity):
    visits, users = routes_t.shape
    clusters = cluster_slot.shape[0]
    ids = lax.broadcasted_iota(jnp.int32, (visits, clusters, users), 1)
    slots = jnp.sum(
        jnp.where(routes_t[:, None, :] == ids, cluster_slot[None, :, None], 0), axis=1
    )
    rows = lax.broadcasted_iota(jnp.int32, (clusters, users), 0)
    columns = lax.broadcasted_iota(jnp.int32, (users, clusters), 1)
    slots_u = slots.T
    member = jnp.zeros((clusters, users), jnp.bool_)
    member_u = jnp.zeros((users, clusters), jnp.bool_)
    target_u = jnp.zeros((users, clusters), jnp.int32)
    for r in range(visits):
        member = member | (slots[r][None, :] == rows)
        same = slots_u[:, r][:, None] == columns
        member_u = member_u | same
        target_u = jnp.where(same, positives[:, r][:, None] + 1, target_u)
    first = lax.broadcasted_iota(jnp.int32, (users, users), 0)
    second = lax.broadcasted_iota(jnp.int32, (users, users), 1)
    rank = jnp.dot(
        member.astype(jnp.bfloat16),
        (first < second).astype(jnp.bfloat16),
        preferred_element_type=jnp.float32,
    )
    rank_u = jnp.dot(
        (second < first).astype(jnp.bfloat16),
        member_u.astype(jnp.bfloat16),
        preferred_element_type=jnp.float32,
    )
    code = jnp.where(member, rank, -1.0).astype(jnp.bfloat16)
    code_u = jnp.where(member_u, rank_u, -1.0)
    seats = [
        jnp.sum(jnp.where(code_u == k, target_u, 0), axis=0) for k in range(capacity)
    ]
    return code, jnp.stack(seats)


def owner(queries, targets, block_items, table_ids, counts):
    clusters, samples = table_ids.shape
    item_rows = block_items.shape[1]
    recip = 1.0 / counts.astype(jnp.float32)
    which = lax.broadcasted_iota(jnp.int32, (clusters, item_rows, samples), 1)
    mass = jnp.sum(jnp.where(table_ids[:, None, :] == which, recip[:, None, :], 0.0), axis=2)
    log_mass = jnp.log(mass)
    lanes = 128
    groups = samples // lanes
    low = targets % lanes
    high = targets // lanes
    pick_low = (
        low[:, :, None] == lax.broadcasted_iota(jnp.int32, low.shape + (lanes,), 2)
    ).astype(jnp.bfloat16)
    table = jnp.concatenate([table_ids, counts // 64, counts % 64], axis=1)
    table = table.reshape(clusters, 3 * groups, lanes).astype(jnp.bfloat16)
    near = jnp.einsum("cql,chl->cqh", pick_low, table, preferred_element_type=jnp.float32)
    column = lax.broadcasted_iota(jnp.int32, near.shape, 2)
    parts = [
        jnp.sum(jnp.where(column == high[:, :, None] + groups * t, near, 0.0), axis=2)
        for t in range(3)
    ]
    live = targets >= 0
    own_id = parts[0].astype(jnp.int32)
    own_count = jnp.where(live, parts[1] * 64.0 + parts[2], 1.0)
    scores = jnp.einsum("cqe,cie->cqi", queries, block_items, preferred_element_type=jnp.float32)
    shifted = scores + log_mass[:, None, :]
    top = jnp.max(shifted, axis=2, keepdims=True)
    expo = jnp.exp(shifted - top)
    total = jnp.sum(expo, axis=2, keepdims=True)
    hit = (
        lax.broadcasted_iota(jnp.int32, scores.shape, 2)
        == jnp.where(live, own_id, -1)[:, :, None]
    )
    picked = jnp.sum(jnp.where(hit, scores, 0.0), axis=2) - jnp.log(own_count)
    losses = jnp.log(total[:, :, 0]) + top[:, :, 0] - picked
    cluster_loss = jnp.sum(jnp.where(live, losses, 0.0), axis=1) / jnp.sum(
        live.astype(jnp.float32), axis=1
    )
    wsum = expo / total - hit.astype(jnp.float32)
    coarse = lax.reduce_precision(wsum, 8, 7)
    fine = (wsum - coarse).astype(jnp.bfloat16)
    coarse = coarse.astype(jnp.bfloat16)

    def both(equation, other):
        return jnp.einsum(
            equation, coarse, other, preferred_element_type=jnp.float32
        ) + jnp.einsum(equation, fine, other, preferred_element_type=jnp.float32)

    dquery = both("cqi,cie->cqe", block_items).astype(jnp.bfloat16)
    dtable = both("cqi,cqe->cie", queries)
    return cluster_loss, dquery, dtable


ORDERS = 3
TILE = 16


def row_groups(bits, tiles):
    turn = [b for b in (1, 2, 3) if b < bits]
    rest = [b for b in range(bits) if b > 3]
    shares = [tiles] if tiles == 1 else [tiles - tiles // 2, tiles // 2]
    groups = []
    start = 0
    for share in shares:
        for k in range(ORDERS):
            k = k % max(1, len(turn))
            size = (share * TILE) << bits
            groups.append((start, size, [0] + turn[k:] + turn[:k] + rest))
            start += size
    return groups


def blocks_of(ref):
    rows, columns = ref.shape
    return [(c, rows) for c in range(columns // 128)]


def reduce_kernel(bits, tiles, big_ref, small_ref, big_out, small_out, acc, out, inbox, full, send, recv):
    me = lax.axis_index("dev")
    mesh = pl.DeviceIdType.MESH
    groups = row_groups(bits, tiles)
    total = groups[-1][0] + groups[-1][1]
    bit = [(me // (1 << b)) % 2 for b in range(bits)]
    partners = [me + (1 << b) * (1 - 2 * bit[b]) for b in range(bits)]

    barrier = pltpu.get_barrier_semaphore()
    for b in range(bits):
        pl.semaphore_signal(barrier, inc=1, device_id=(partners[b],), device_id_type=mesh)
    row = 0
    for ref in (big_ref, small_ref):
        for c, rows in blocks_of(ref):
            acc[row : row + rows, :] = ref[:, c * 128 : (c + 1) * 128]
            row += rows
    if row < total:
        acc[row:, :] = jnp.zeros((total - row, 128), jnp.float32)

    def rows_at(first, count):
        return pl.ds(pl.multiple_of(first, TILE), count)

    off = [start for start, _, _ in groups]
    length = [size for _, size, _ in groups]
    waiting = [None] * len(groups)
    landed = [0] * len(groups)
    started = []

    def take(g):
        waiting[g].wait_recv()
        kept = rows_at(off[g], length[g])
        got = inbox[pl.ds(groups[g][0] + landed[g], length[g]), :].astype(jnp.float32)
        acc[kept, :] = acc[kept, :] + got
        landed[g] += length[g]

    for s in range(bits):
        for g in range(len(groups)):
            start, _, order = groups[g]
            if s > 0:
                take(g)
            b = order[s]
            half = length[g] // 2
            give = off[g] + (1 - bit[b]) * half
            off[g] = off[g] + bit[b] * half
            length[g] = half
            out[rows_at(give, half), :] = acc[rows_at(give, half), :].astype(jnp.bfloat16)
            if s == 0 and g == 0:
                pl.semaphore_wait(barrier, bits)
            copy = pltpu.make_async_remote_copy(
                src_ref=out.at[rows_at(give, half), :],
                dst_ref=inbox.at[pl.ds(start + landed[g], half), :],
                send_sem=send.at[g, s],
                recv_sem=recv.at[g, s],
                device_id=(partners[b],),
                device_id_type=mesh,
            )
            copy.start()
            waiting[g] = copy
            started.append(copy)
    for s in range(bits - 1, -1, -1):
        for g in range(len(groups)):
            if s == bits - 1:
                take(g)
                kept = rows_at(off[g], length[g])
                full[kept, :] = acc[kept, :].astype(jnp.bfloat16)
            else:
                waiting[g].wait_recv()
            b = groups[g][2][s]
            held = rows_at(off[g], length[g])
            copy = pltpu.make_async_remote_copy(
                src_ref=full.at[held, :],
                dst_ref=full.at[held, :],
                send_sem=send.at[g, bits + s],
                recv_sem=recv.at[g, bits + s],
                device_id=(partners[b],),
                device_id_type=mesh,
            )
            copy.start()
            waiting[g] = copy
            started.append(copy)
            off[g] = off[g] - bit[b] * length[g]
            length[g] = length[g] * 2
    for copy in waiting:
        copy.wait_recv()
    for copy in started:
        copy.wait_send()
    row = 0
    for ref in (big_out, small_out):
        for c, rows in blocks_of(ref):
            ref[:, c * 128 : (c + 1) * 128] = full[row : row + rows, :]
            row += rows


def sum_over_devices(big, small):
    devices = lax.axis_size("dev")
    bits = devices.bit_length() - 1
    tiles = -(-((big.size + small.size) // 128) // (ORDERS * devices * TILE))
    groups = row_groups(bits, tiles)
    rows = groups[-1][0] + groups[-1][1]
    summed = pl.pallas_call(
        functools.partial(reduce_kernel, bits, tiles),
        out_shape=(
            jax.ShapeDtypeStruct(big.shape, jnp.bfloat16),
            jax.ShapeDtypeStruct(small.shape, jnp.bfloat16),
        ),
        in_specs=[pl.BlockSpec(memory_space=pltpu.VMEM)] * 2,
        out_specs=[pl.BlockSpec(memory_space=pltpu.VMEM)] * 2,
        scratch_shapes=[
            pltpu.VMEM((rows, 128), jnp.float32),
            pltpu.VMEM((rows, 128), jnp.bfloat16),
            pltpu.VMEM((rows, 128), jnp.bfloat16),
            pltpu.VMEM((rows, 128), jnp.bfloat16),
            pltpu.SemaphoreType.DMA((len(groups), 2 * bits)),
            pltpu.SemaphoreType.DMA((len(groups), 2 * bits)),
        ],
        compiler_params=pltpu.CompilerParams(collective_id=0, has_side_effects=True),
        name="sum_over_devices",
    )(big, small)
    return tuple(part.astype(jnp.float32) for part in summed)


def local(
    features, w_hidden, w_out, items, routes, cluster_slot, sample_ids, sample_counts, positives
):
    devices = lax.axis_size("dev")
    users, visits = routes.shape
    clusters = cluster_slot.shape[0]
    local_clusters = sample_ids.shape[0]
    width = w_out.shape[1]
    item_rows = items.shape[0] // local_clusters
    capacity = max(2, 2 * users * visits // (local_clusters * devices))
    rows = local_clusters * capacity
    code, send_target = slot_codes(routes.T, positives, cluster_slot, capacity)
    seats = lax.broadcasted_iota(jnp.int32, (1, capacity, 1), 1).astype(jnp.bfloat16)
    seated = code[:, None, :] == seats
    select = seated.astype(jnp.bfloat16).reshape(clusters * capacity, users)
    send_target = send_target.reshape(capacity, devices, local_clusters)
    send_target = send_target.transpose(1, 0, 2).reshape(devices, rows)
    coded = jnp.concatenate([send_target // 64, send_target % 64], axis=1)
    extra = -(-coded.shape[1] // (8 * width)) * 8
    coded = jnp.pad(coded, ((0, 0), (0, extra * width - coded.shape[1])))
    coded = coded.astype(jnp.bfloat16).reshape(devices, extra, width)
    pre = jnp.dot(features, w_hidden, preferred_element_type=jnp.float32)
    hidden = jax.nn.silu(pre).astype(jnp.bfloat16)
    query = jnp.dot(hidden, w_out, preferred_element_type=jnp.float32).astype(jnp.bfloat16)
    send_query = jnp.dot(select, query, preferred_element_type=jnp.float32).astype(jnp.bfloat16)
    payload = jnp.concatenate([send_query.reshape(devices, rows, width), coded], axis=1)
    got = lax.all_to_all(payload, "dev", split_axis=0, concat_axis=0, tiled=True)
    got_query = got[:, :rows].reshape(devices, local_clusters, capacity, width)
    got_query = got_query.transpose(1, 0, 2, 3).reshape(local_clusters, devices * capacity, width)
    got_coded = got[:, rows:].reshape(devices, extra * width).astype(jnp.int32)
    got_target = got_coded[:, :rows] * 64 + got_coded[:, rows : 2 * rows] - 1
    got_target = got_target.reshape(devices, capacity, local_clusters)
    got_target = got_target.transpose(2, 0, 1).reshape(local_clusters, devices * capacity)
    slot_loss, dquery, dtable = owner(
        got_query,
        got_target,
        items.reshape(local_clusters, item_rows, width),
        sample_ids,
        sample_counts,
    )
    back = dquery.reshape(local_clusters, devices, capacity, width).transpose(1, 0, 2, 3)
    returned = lax.all_to_all(
        back.reshape(devices, rows, width), "dev", split_axis=0, concat_axis=0, tiled=True
    ).reshape(clusters * capacity, width)
    dq_total = lax.dot_general(
        select, returned, (((0,), (0,)), ((), ())), preferred_element_type=jnp.float32
    ).astype(jnp.bfloat16)
    local_out = jnp.dot(hidden.T, dq_total, preferred_element_type=jnp.float32)
    dhidden = jnp.dot(dq_total, w_out.T, preferred_element_type=jnp.float32)
    dpre = (dhidden * silu_grad(pre)).astype(jnp.bfloat16)
    local_hidden = jnp.dot(features.T, dpre, preferred_element_type=jnp.float32)
    grad_hidden, grad_out = sum_over_devices(local_hidden, local_out)
    return (slot_loss, grad_hidden, grad_out, dtable.reshape(items.shape[0], width))


def solution(mesh):
    in_specs = (
        P("dev", None),
        P(),
        P(),
        P("dev", None),
        P("dev", None),
        P(),
        P("dev", None),
        P("dev", None),
        P("dev", None),
    )
    out_specs = (P("dev"), P(), P(), P("dev", None))
    return jax.shard_map(local, mesh=mesh, in_specs=in_specs, out_specs=out_specs, check_vma=False)
```

```python
import functools

import jax
import jax.numpy as jnp
from jax import lax
from jax.experimental import pallas as pl
from jax.experimental.pallas import tpu as pltpu
from jax.sharding import PartitionSpec as P


def silu_grad(value):
    sig = jax.nn.sigmoid(value)
    return sig * (1.0 + value * (1.0 - sig))


def slot_codes(routes_t, positives, cluster_slot, capacity):
    visits, users = routes_t.shape
    clusters = cluster_slot.shape[0]
    ids = lax.broadcasted_iota(jnp.int32, (visits, clusters, users), 1)
    slots = jnp.sum(
        jnp.where(routes_t[:, None, :] == ids, cluster_slot[None, :, None], 0), axis=1
    )
    rows = lax.broadcasted_iota(jnp.int32, (clusters, users), 0)
    columns = lax.broadcasted_iota(jnp.int32, (users, clusters), 1)
    slots_u = slots.T
    member = jnp.zeros((clusters, users), jnp.bool_)
    member_u = jnp.zeros((users, clusters), jnp.bool_)
    target_u = jnp.zeros((users, clusters), jnp.int32)
    for r in range(visits):
        member = member | (slots[r][None, :] == rows)
        same = slots_u[:, r][:, None] == columns
        member_u = member_u | same
        target_u = jnp.where(same, positives[:, r][:, None] + 1, target_u)
    first = lax.broadcasted_iota(jnp.int32, (users, users), 0)
    second = lax.broadcasted_iota(jnp.int32, (users, users), 1)
    rank = jnp.dot(
        member.astype(jnp.bfloat16),
        (first < second).astype(jnp.bfloat16),
        preferred_element_type=jnp.float32,
    )
    rank_u = jnp.dot(
        (second < first).astype(jnp.bfloat16),
        member_u.astype(jnp.bfloat16),
        preferred_element_type=jnp.float32,
    )
    code = jnp.where(member, rank, -1.0).astype(jnp.bfloat16)
    code_u = jnp.where(member_u, rank_u, -1.0)
    seats = lax.broadcasted_iota(jnp.int32, (capacity, 1, 1), 0).astype(jnp.float32)
    return code, jnp.sum(jnp.where(code_u[None] == seats, target_u[None], 0), axis=1)


def owner(queries, targets, block_items, table_ids, counts):
    clusters, samples = table_ids.shape
    item_rows = block_items.shape[1]
    recip = 1.0 / counts.astype(jnp.float32)
    which = lax.broadcasted_iota(jnp.int32, (clusters, item_rows, samples), 1)
    mass = jnp.sum(jnp.where(table_ids[:, None, :] == which, recip[:, None, :], 0.0), axis=2)
    log_mass = jnp.log(mass)
    lanes = 128
    groups = samples // lanes
    low = targets % lanes
    high = targets // lanes
    pick_low = (
        low[:, :, None] == lax.broadcasted_iota(jnp.int32, low.shape + (lanes,), 2)
    ).astype(jnp.bfloat16)
    table = jnp.concatenate([table_ids, counts // 64, counts % 64], axis=1)
    table = table.reshape(clusters, 3 * groups, lanes).astype(jnp.bfloat16)
    near = jnp.einsum("cql,chl->cqh", pick_low, table, preferred_element_type=jnp.float32)
    column = lax.broadcasted_iota(jnp.int32, near.shape, 2)
    parts = [
        jnp.sum(jnp.where(column == high[:, :, None] + groups * t, near, 0.0), axis=2)
        for t in range(3)
    ]
    live = targets >= 0
    own_id = parts[0].astype(jnp.int32)
    own_count = jnp.where(live, parts[1] * 64.0 + parts[2], 1.0)
    scores = jnp.einsum("cqe,cie->cqi", queries, block_items, preferred_element_type=jnp.float32)
    shifted = scores + log_mass[:, None, :]
    top = jnp.max(shifted, axis=2, keepdims=True)
    expo = jnp.exp(shifted - top)
    total = jnp.sum(expo, axis=2, keepdims=True)
    hit = (
        lax.broadcasted_iota(jnp.int32, scores.shape, 2)
        == jnp.where(live, own_id, -1)[:, :, None]
    )
    picked = jnp.sum(jnp.where(hit, scores, 0.0), axis=2) - jnp.log(own_count)
    losses = jnp.log(total[:, :, 0]) + top[:, :, 0] - picked
    cluster_loss = jnp.sum(jnp.where(live, losses, 0.0), axis=1) / jnp.sum(
        live.astype(jnp.float32), axis=1
    )
    wsum = expo / total - hit.astype(jnp.float32)
    coarse = lax.reduce_precision(wsum, 8, 7)
    fine = (wsum - coarse).astype(jnp.bfloat16)
    coarse = coarse.astype(jnp.bfloat16)

    def both(equation, other):
        return jnp.einsum(
            equation, coarse, other, preferred_element_type=jnp.float32
        ) + jnp.einsum(equation, fine, other, preferred_element_type=jnp.float32)

    dquery = both("cqi,cie->cqe", block_items).astype(jnp.bfloat16)
    dtable = both("cqi,cqe->cie", queries)
    return cluster_loss, dquery, dtable


ORDERS = 3
TILE = 16


def row_groups(bits, tiles):
    turn = [b for b in (1, 2, 3) if b < bits]
    rest = [b for b in range(bits) if b > 3]
    shares = [tiles] if tiles == 1 else [tiles - tiles // 2, tiles // 2]
    groups = []
    start = 0
    for share in shares:
        for k in range(ORDERS):
            k = k % max(1, len(turn))
            size = (share * TILE) << bits
            groups.append((start, size, [0] + turn[k:] + turn[:k] + rest))
            start += size
    return groups


def pieces_of(refs, start, size):
    row = 0
    for ref in refs:
        rows, columns = ref.shape
        for c in range(columns // 128):
            low, high = max(start, row), min(start + size, row + rows)
            if low < high:
                yield low, high, ref.at[low - row : high - row, c * 128 : (c + 1) * 128]
            row += rows
    low = max(start, row)
    if low < start + size:
        yield low, start + size, None


def reduce_kernel(bits, tiles, big_ref, small_ref, big_out, small_out, acc, out, inbox, full, send, recv):
    me = lax.axis_index("dev")
    mesh = pl.DeviceIdType.MESH
    groups = row_groups(bits, tiles)
    bit = [(me // (1 << b)) % 2 for b in range(bits)]
    partners = [me + (1 << b) * (1 - 2 * bit[b]) for b in range(bits)]

    barrier = pltpu.get_barrier_semaphore()
    for b in range(bits):
        pl.semaphore_signal(barrier, inc=1, device_id=(partners[b],), device_id_type=mesh)
    def rows_at(first, count):
        return pl.ds(pl.multiple_of(first, TILE), count)

    off = [start for start, _, _ in groups]
    length = [size for _, size, _ in groups]
    waiting = [None] * len(groups)
    landed = [0] * len(groups)
    started = []

    def take(g):
        waiting[g].wait_recv()
        kept = rows_at(off[g], length[g])
        got = inbox[pl.ds(groups[g][0] + landed[g], length[g]), :].astype(jnp.float32)
        acc[kept, :] = acc[kept, :] + got
        landed[g] += length[g]

    for s in range(bits):
        for g in range(len(groups)):
            start, size, order = groups[g]
            if s > 0:
                take(g)
            else:
                for low, high, part in pieces_of((big_ref, small_ref), start, size):
                    blank = jnp.zeros((high - low, 128), jnp.float32)
                    acc[low:high, :] = blank if part is None else part[...]
            b = order[s]
            half = length[g] // 2
            give = off[g] + (1 - bit[b]) * half
            off[g] = off[g] + bit[b] * half
            length[g] = half
            out[rows_at(give, half), :] = acc[rows_at(give, half), :].astype(jnp.bfloat16)
            if s == 0 and g == 0:
                pl.semaphore_wait(barrier, bits)
            copy = pltpu.make_async_remote_copy(
                src_ref=out.at[rows_at(give, half), :],
                dst_ref=inbox.at[pl.ds(start + landed[g], half), :],
                send_sem=send.at[g, s],
                recv_sem=recv.at[g, s],
                device_id=(partners[b],),
                device_id_type=mesh,
            )
            copy.start()
            waiting[g] = copy
            started.append(copy)
    for s in range(bits - 1, -1, -1):
        for g in range(len(groups)):
            if s == bits - 1:
                take(g)
                kept = rows_at(off[g], length[g])
                full[kept, :] = acc[kept, :].astype(jnp.bfloat16)
            else:
                waiting[g].wait_recv()
            b = groups[g][2][s]
            held = rows_at(off[g], length[g])
            copy = pltpu.make_async_remote_copy(
                src_ref=full.at[held, :],
                dst_ref=full.at[held, :],
                send_sem=send.at[g, bits + s],
                recv_sem=recv.at[g, bits + s],
                device_id=(partners[b],),
                device_id_type=mesh,
            )
            copy.start()
            waiting[g] = copy
            started.append(copy)
            off[g] = off[g] - bit[b] * length[g]
            length[g] = length[g] * 2
    for g in range(len(groups)):
        waiting[g].wait_recv()
        for low, high, part in pieces_of((big_out, small_out), groups[g][0], groups[g][1]):
            if part is not None:
                part[...] = full[low:high, :]
    for copy in started:
        copy.wait_send()


def sum_over_devices(big, small):
    devices = lax.axis_size("dev")
    bits = devices.bit_length() - 1
    tiles = -(-((big.size + small.size) // 128) // (ORDERS * devices * TILE))
    groups = row_groups(bits, tiles)
    rows = groups[-1][0] + groups[-1][1]
    summed = pl.pallas_call(
        functools.partial(reduce_kernel, bits, tiles),
        out_shape=(
            jax.ShapeDtypeStruct(big.shape, jnp.bfloat16),
            jax.ShapeDtypeStruct(small.shape, jnp.bfloat16),
        ),
        in_specs=[pl.BlockSpec(memory_space=pltpu.VMEM)] * 2,
        out_specs=[pl.BlockSpec(memory_space=pltpu.VMEM)] * 2,
        scratch_shapes=[
            pltpu.VMEM((rows, 128), jnp.float32),
            pltpu.VMEM((rows, 128), jnp.bfloat16),
            pltpu.VMEM((rows, 128), jnp.bfloat16),
            pltpu.VMEM((rows, 128), jnp.bfloat16),
            pltpu.SemaphoreType.DMA((len(groups), 2 * bits)),
            pltpu.SemaphoreType.DMA((len(groups), 2 * bits)),
        ],
        compiler_params=pltpu.CompilerParams(collective_id=0, has_side_effects=True),
        name="sum_over_devices",
    )(big, small)
    return tuple(part.astype(jnp.float32) for part in summed)


def local(
    features, w_hidden, w_out, items, routes, cluster_slot, sample_ids, sample_counts, positives
):
    devices = lax.axis_size("dev")
    users, visits = routes.shape
    clusters = cluster_slot.shape[0]
    local_clusters = sample_ids.shape[0]
    width = w_out.shape[1]
    item_rows = items.shape[0] // local_clusters
    capacity = max(2, 2 * users * visits // (local_clusters * devices))
    rows = local_clusters * capacity
    code, send_target = slot_codes(routes.T, positives, cluster_slot, capacity)
    seats = lax.broadcasted_iota(jnp.int32, (1, capacity, 1), 1).astype(jnp.bfloat16)
    seated = code[:, None, :] == seats
    select = seated.astype(jnp.bfloat16).reshape(clusters * capacity, users)
    send_target = send_target.reshape(capacity, devices, local_clusters)
    send_target = send_target.transpose(1, 0, 2).reshape(devices, rows)
    coded = jnp.concatenate([send_target // 64, send_target % 64], axis=1)
    extra = -(-coded.shape[1] // (8 * width)) * 8
    coded = jnp.pad(coded, ((0, 0), (0, extra * width - coded.shape[1])))
    coded = coded.astype(jnp.bfloat16).reshape(devices, extra, width)
    pre = jnp.dot(features, w_hidden, preferred_element_type=jnp.float32)
    hidden = jax.nn.silu(pre).astype(jnp.bfloat16)
    query = jnp.dot(hidden, w_out, preferred_element_type=jnp.float32).astype(jnp.bfloat16)
    send_query = jnp.dot(select, query, preferred_element_type=jnp.float32).astype(jnp.bfloat16)
    payload = jnp.concatenate([send_query.reshape(devices, rows, width), coded], axis=1)
    got = lax.all_to_all(payload, "dev", split_axis=0, concat_axis=0, tiled=True)
    got_query = got[:, :rows].reshape(devices, local_clusters, capacity, width)
    got_query = got_query.transpose(1, 0, 2, 3).reshape(local_clusters, devices * capacity, width)
    got_coded = got[:, rows:].reshape(devices, extra * width).astype(jnp.int32)
    got_target = got_coded[:, :rows] * 64 + got_coded[:, rows : 2 * rows] - 1
    got_target = got_target.reshape(devices, capacity, local_clusters)
    got_target = got_target.transpose(2, 0, 1).reshape(local_clusters, devices * capacity)
    slot_loss, dquery, dtable = owner(
        got_query,
        got_target,
        items.reshape(local_clusters, item_rows, width),
        sample_ids,
        sample_counts,
    )
    back = dquery.reshape(local_clusters, devices, capacity, width).transpose(1, 0, 2, 3)
    returned = lax.all_to_all(
        back.reshape(devices, rows, width), "dev", split_axis=0, concat_axis=0, tiled=True
    ).reshape(clusters * capacity, width)
    dq_total = lax.dot_general(
        select, returned, (((0,), (0,)), ((), ())), preferred_element_type=jnp.float32
    ).astype(jnp.bfloat16)
    local_out = jnp.dot(hidden.T, dq_total, preferred_element_type=jnp.float32)
    dhidden = jnp.dot(dq_total, w_out.T, preferred_element_type=jnp.float32)
    dpre = (dhidden * silu_grad(pre)).astype(jnp.bfloat16)
    local_hidden = jnp.dot(features.T, dpre, preferred_element_type=jnp.float32)
    grad_hidden, grad_out = sum_over_devices(local_hidden, local_out)
    return (slot_loss, grad_hidden, grad_out, dtable.reshape(items.shape[0], width))


def solution(mesh):
    in_specs = (
        P("dev", None),
        P(),
        P(),
        P("dev", None),
        P("dev", None),
        P(),
        P("dev", None),
        P("dev", None),
        P("dev", None),
    )
    out_specs = (P("dev"), P(), P(), P("dev", None))
    return jax.shard_map(local, mesh=mesh, in_specs=in_specs, out_specs=out_specs, check_vma=False)
```
